32 devices in a mesh: pi: 4 (over x, core), pj: 8 (over z, y).
Axes of the slice: x: 2, y: 2, z: 4, core: 2. Of those that a mesh axis runs over, the one named last changes fastest.
Arguments:
- amplitudes: bfloat16 [8, 8, 128, 128], P('pi', 'pj'), may hold values from -6 to 6
- cholesky: bfloat16 [128, 128, 4096], P(None, None, 'pj'), may hold values from -1 to 1, as said below
- other_terms: float32 [8, 8, 128, 128], P('pi', 'pj'), may hold values from -6 to 6
Outputs:
- residual: float32 [8, 8, 128, 128], P('pi', 'pj')
The draws below stay inside these ranges and needn't reach their ends.
Inputs may be any that keep to these rules, and one draw needn't show every extreme that they name: cholesky[x, y, P] equals cholesky[y, x, P].
All inputs are finite; a program needn't handle non-finite values.
Results may differ from the reference program's by a relative error of at most 0.0036.
Values may be sent and summed in bfloat16 or wider, within the bound.
No kernel may reach another device: no remote copies, remote signals or barrier semaphores. Data moves between devices by JAX's collectives and lax.ppermute only.
A program may use at most 128 MiB of HBM per device.

```python
import math
import jax
import jax.numpy as jnp
from jax import lax

NV = 128
NCHOL = 4096
NOCC = 8


def draw_cholesky(key, part):
    scale = 1.0 / math.sqrt(NV * math.sqrt(NCHOL))
    base = jax.random.truncated_normal(key, -6.0, 6.0, (NV, NV, NCHOL), jnp.float32)
    sym = (base + jnp.swapaxes(base, 0, 1)) * (scale / math.sqrt(2.0))
    return sym.astype(jnp.bfloat16)


def shard_levels(stream_key, extent, pieces, smallest, largest):
    def one(axis_at, parts):
        heights = jax.random.uniform(jax.random.fold_in(jax.random.fold_in(stream_key, 6), axis_at), (parts,), jnp.float32, smallest / len(pieces), largest / len(pieces))
        return jnp.repeat(jnp.exp(heights), extent[axis_at] // parts).reshape((-1,) + (1,) * (len(extent) - axis_at - 1))

    level = one(*pieces[0])
    for cut in pieces[1:]:
        level = level * one(*cut)
    return level


def scatter_about(rng, shape, spread, limit, pieces=(), kind=jnp.bfloat16):
    entries = spread * jax.random.normal(rng, shape, jnp.float32)
    if pieces:
        entries = entries * shard_levels(rng, shape, pieces, -0.22, 0.18)
    return jnp.clip(entries, -limit, limit).astype(kind)


def setup_inputs(seed: int = 0) -> dict:
    arg_keys = jax.random.split(jax.random.key(seed), 4)
    return {
        "amplitudes": scatter_about(arg_keys[0], (NOCC, NOCC, NV, NV), 1.0, 6.0, ((0, 4), (1, 8))),
        "cholesky": draw_cholesky(jax.random.fold_in(arg_keys[3], 71), 0),
        "other_terms": scatter_about(arg_keys[2], (NOCC, NOCC, NV, NV), 1.0, 6.0, ((0, 4), (1, 8)), jnp.float32),
    }


def reference(amplitudes, cholesky, other_terms):
    vectors = cholesky.astype(jnp.float32)
    pairs = amplitudes.astype(jnp.float32)

    def one_virtual(index):
        left = lax.dynamic_index_in_dim(vectors, index, 0, keepdims=False)
        tile = jnp.einsum("cp,bdp->bcd", left, vectors).astype(jnp.bfloat16)
        tile = lax.optimization_barrier(tile).astype(jnp.float32)
        return jnp.einsum("ijcd,bcd->ijb", pairs, tile)

    stacked = lax.map(one_virtual, jnp.arange(NV, dtype=jnp.int32))
    ladder = jnp.transpose(stacked, (1, 2, 0, 3))
    half = (other_terms + 0.5 * ladder).astype(jnp.bfloat16)
    wide = lax.optimization_barrier(half).astype(jnp.float32)
    return wide + jnp.transpose(wide, (1, 0, 3, 2))
```

```python
import functools

import jax
import jax.numpy as jnp
from jax import lax
from jax.experimental import pallas as pl
from jax.experimental.pallas import tpu as pltpu
from jax.sharding import PartitionSpec as P


BOTH = ("pi", "pj")
GROUP = 16
NT = (((1,), (1,)), ((), ()))
NN = (((1,), (0,)), ((), ()))
ANY = pl.BlockSpec(memory_space=pl.ANY)
VMEM = pl.BlockSpec(memory_space=pltpu.VMEM)


def mirrored(block):
    pair_i = block.shape[0]
    count_i, count_j = lax.axis_size("pi"), lax.axis_size("pj")
    col = lax.axis_index("pj")
    arrived = []
    for shift in range(pair_i):
        route = []
        for row in range(count_i):
            for at in range(count_j):
                to = (at // pair_i) * count_j + pair_i * row + (at + shift) % pair_i
                route.append((row * count_j + at, to))
        sent = lax.dynamic_index_in_dim(block, (col + shift) % pair_i, 0, keepdims=False)
        arrived.append(lax.ppermute(sent, BOTH, route))
    stacked = jnp.stack(arrived)
    return jnp.stack(
        [
            lax.dynamic_index_in_dim(stacked, (col - slot) % pair_i, 0, keepdims=False)
            for slot in range(pair_i)
        ]
    )


def packed(pairs):
    width = pairs.shape[-1]
    total = jnp.swapaxes(pairs, 1, 2).astype(jnp.float32) + mirrored(pairs).astype(jnp.float32)
    d = lax.broadcasted_iota(jnp.int32, (width, width), 0)
    c = lax.broadcasted_iota(jnp.int32, (width, width), 1)
    weight = jnp.where(c < d, 1.0, jnp.where(c == d, 0.5, 0.0))
    total = (total * weight).astype(jnp.bfloat16)
    parts = []
    for low in range(0, width, GROUP):
        high = low + GROUP
        parts.append(total[:, low:high, :high].reshape(pairs.shape[0], GROUP * high))
    return jnp.concatenate(parts, axis=1)


def offsets(width):
    at = [0]
    for k in range(width // GROUP):
        at.append(at[-1] + GROUP * GROUP * (k + 1))
    return at


def load(start, rows, l_hbm, own, vectors, sems):
    blocks = vectors.shape[0] // GROUP
    copies = [pltpu.make_async_copy(l_hbm.at[pl.ds(start, rows)], own, sems.at[blocks])]
    for k in range(blocks):
        part = pl.ds(k * GROUP, GROUP)
        copies.append(pltpu.make_async_copy(l_hbm.at[part], vectors.at[part], sems.at[k]))
    for copy in copies:
        copy.start()
    return copies


def form(own, vectors, at, chunk, k, store):
    width, _, depth = vectors.shape
    high = GROUP * (k + 1)
    left = own[pl.ds(at * chunk, chunk), :high, :].reshape(chunk * high, depth)
    for pair in range(0, GROUP, 2):
        right = vectors[pl.ds(k * GROUP + pair, 2)].reshape(2 * width, depth)
        product = lax.dot_general(left, right, NT, preferred_element_type=jnp.float32)
        product = product.astype(jnp.bfloat16)
        for q in range(2):
            part = product[:, q * width : (q + 1) * width].reshape(chunk, high, width)
            store(pl.ds((pair + q) * high, high), part)


def tile_kernel(rows, chunk, start_ref, l_hbm, t_hbm, vectors, own, tile, sems, sent):
    width = vectors.shape[0]
    blocks = width // GROUP
    at_row = offsets(width)
    copies = load(start_ref[0], rows, l_hbm, own, vectors, sems)
    copies[0].wait()

    def out_copy(at, k):
        size = at_row[k + 1] - at_row[k]
        return pltpu.make_async_copy(
            tile.at[k % 2, :, pl.ds(0, size)],
            t_hbm.at[pl.ds(at * chunk, chunk), pl.ds(at_row[k], size)],
            sent.at[k % 2],
        )

    def step(at, carry):
        for k in range(blocks):
            pl.when(at == 0)(copies[k + 1].wait)
            if k >= 2:
                out_copy(at, k - 2).wait()
            else:
                pl.when(at > 0)(out_copy(at - 1, blocks - 2 + k).wait)

            def store(part, value, k=k):
                tile[k % 2, :, part] = value

            form(own, vectors, at, chunk, k, store)
            out_copy(at, k).start()
        return carry

    lax.fori_loop(0, rows // chunk, step, 0)
    last = rows // chunk - 1
    out_copy(last, blocks - 2).wait()
    out_copy(last, blocks - 1).wait()


def tiles(cholesky, start, rows):
    width, _, depth = cholesky.shape
    chunk = min(8, rows)
    size = offsets(width)[-1]
    return pl.pallas_call(
        functools.partial(tile_kernel, rows, chunk),
        out_shape=jax.ShapeDtypeStruct((rows, size, width), jnp.bfloat16),
        grid_spec=pltpu.PrefetchScalarGridSpec(
            num_scalar_prefetch=1,
            grid=(),
            in_specs=[ANY],
            out_specs=ANY,
            scratch_shapes=[
                pltpu.VMEM((width, width, depth), jnp.bfloat16),
                pltpu.VMEM((rows, width, depth), jnp.bfloat16),
                pltpu.VMEM((2, chunk, GROUP * width, width), jnp.bfloat16),
                pltpu.SemaphoreType.DMA((width // GROUP + 1,)),
                pltpu.SemaphoreType.DMA((2,)),
            ],
        ),
        compiler_params=pltpu.CompilerParams(vmem_limit_bytes=56 << 20),
        cost_estimate=pl.CostEstimate(
            flops=2 * rows * width * size * depth,
            bytes_accessed=2 * width * width * depth + 2 * rows * size * width,
            transcendentals=0,
        ),
    )(start, cholesky)


def apply_kernel(t_ref, s_ref, out_ref):
    for a in range(t_ref.shape[0]):
        out_ref[a] = lax.dot_general(s_ref[...], t_ref[a], NN, preferred_element_type=jnp.float32)


def applied(tile, weights):
    rows, size, width = tile.shape
    pairs = weights.shape[0]
    each = 2 if rows % 2 == 0 else 1
    return pl.pallas_call(
        apply_kernel,
        out_shape=jax.ShapeDtypeStruct((rows, pairs, width), jnp.float32),
        grid=(rows // each,),
        in_specs=[pl.BlockSpec((each, size, width), lambda a: (a, 0, 0)), VMEM],
        out_specs=pl.BlockSpec((each, pairs, width), lambda a: (a, 0, 0)),
        compiler_params=pltpu.CompilerParams(vmem_limit_bytes=56 << 20),
        cost_estimate=pl.CostEstimate(
            flops=2 * rows * width * size * pairs,
            bytes_accessed=2 * rows * size * width,
            transcendentals=0,
        ),
    )(tile, weights)


def ladder_kernel(rows, chunk, start_ref, l_hbm, s_ref, out_ref, vectors, own, tile, sems):
    width = vectors.shape[0]
    blocks = width // GROUP
    at_row = offsets(width)
    copies = load(start_ref[0], rows, l_hbm, own, vectors, sems)
    copies[0].wait()

    def step(at, carry):
        for k in range(blocks):
            pl.when(at == 0)(copies[k + 1].wait)

            def store(part, value):
                tile[:, part] = value

            form(own, vectors, at, chunk, k, store)
            weights = s_ref[:, at_row[k] : at_row[k + 1]]
            for a in range(chunk):
                value = lax.dot_general(
                    weights,
                    tile[a, : at_row[k + 1] - at_row[k], :],
                    NN,
                    preferred_element_type=jnp.float32,
                )
                if k == 0:
                    out_ref[at * chunk + a] = value
                else:
                    out_ref[at * chunk + a] += value
        return carry

    lax.fori_loop(0, rows // chunk, step, 0)


def ladder(cholesky, weights, start, rows):
    width, _, depth = cholesky.shape
    pairs, size = weights.shape
    chunk = min(8, rows)
    return pl.pallas_call(
        functools.partial(ladder_kernel, rows, chunk),
        out_shape=jax.ShapeDtypeStruct((rows, pairs, width), jnp.float32),
        grid_spec=pltpu.PrefetchScalarGridSpec(
            num_scalar_prefetch=1,
            grid=(),
            in_specs=[ANY, VMEM],
            out_specs=VMEM,
            scratch_shapes=[
                pltpu.VMEM((width, width, depth), jnp.bfloat16),
                pltpu.VMEM((rows, width, depth), jnp.bfloat16),
                pltpu.VMEM((chunk, GROUP * width, width), jnp.bfloat16),
                pltpu.SemaphoreType.DMA((width // GROUP + 1,)),
            ],
        ),
        compiler_params=pltpu.CompilerParams(vmem_limit_bytes=56 << 20),
        cost_estimate=pl.CostEstimate(
            flops=2 * rows * width * size * (depth + pairs),
            bytes_accessed=2 * width * width * depth,
            transcendentals=0,
        ),
    )(start, cholesky, weights)


def sent(sums, after=None):
    sums = jnp.swapaxes(sums, 0, 1).astype(jnp.bfloat16)
    if after is not None:
        sums, after = lax.optimization_barrier((sums, after))
    return lax.all_to_all(sums, BOTH, split_axis=0, concat_axis=0, tiled=True), after


def collected(landed):
    count_i, count_j = lax.axis_size("pi"), lax.axis_size("pj")
    landed = landed.reshape((count_i, count_j, -1) + landed.shape[1:]).astype(jnp.float32)
    return jnp.sum(landed, axis=1)


def shards(amplitudes, cholesky, other_terms):
    width = cholesky.shape[0]
    pair_i, pair_j = amplitudes.shape[:2]
    count_i, count_j = lax.axis_size("pi"), lax.axis_size("pj")
    devices = count_i * count_j
    assert pair_j == 1 and pair_i * count_i == count_j
    rows = width // count_i
    early = rows - rows // 4 if rows % 32 == 0 else rows // 2
    start = lax.axis_index("pi") * rows
    own = packed(amplitudes.reshape(pair_i, width, width))
    copies = jnp.broadcast_to(own[None], (devices,) + own.shape).reshape(devices * pair_i, -1)
    weights = lax.all_to_all(copies, BOTH, split_axis=0, concat_axis=0, tiled=True)
    tile = tiles(cholesky, start.reshape(1), early)
    sums = applied(tile, weights)
    first, _ = sent(sums)
    sums = ladder(cholesky, weights, (start + early).reshape(1), rows - early)
    second, first = sent(sums, first)
    part = jnp.concatenate([collected(first), collected(second)], axis=2)
    part = jnp.swapaxes(part, 0, 1).reshape(pair_i, width, width)
    half = other_terms.reshape(pair_i, width, width) + 0.5 * part
    back = mirrored(half.astype(jnp.bfloat16))
    total = half + jnp.swapaxes(back, 1, 2).astype(jnp.float32)
    return total.reshape(other_terms.shape)


def solution(mesh):
    return jax.shard_map(
        shards,
        mesh=mesh,
        in_specs=(P("pi", "pj", None, None), P(None, None, "pj"), P("pi", "pj", None, None)),
        out_specs=P("pi", "pj", None, None),
        check_vma=False,
    )
```

```python
import functools

import jax
import jax.numpy as jnp
from jax import lax
from jax.experimental import pallas as pl
from jax.experimental.pallas import tpu as pltpu
from jax.sharding import PartitionSpec as P


BOTH = ("pi", "pj")
GROUP = 16
NT = (((1,), (1,)), ((), ()))
NN = (((1,), (0,)), ((), ()))
ANY = pl.BlockSpec(memory_space=pl.ANY)
VMEM = pl.BlockSpec(memory_space=pltpu.VMEM)


def mirrored(block):
    pair_i = block.shape[0]
    count_i, count_j = lax.axis_size("pi"), lax.axis_size("pj")
    col = lax.axis_index("pj")
    arrived = []
    for shift in range(pair_i):
        route = []
        for row in range(count_i):
            for at in range(count_j):
                to = (at // pair_i) * count_j + pair_i * row + (at + shift) % pair_i
                route.append((row * count_j + at, to))
        sent = lax.dynamic_index_in_dim(block, (col + shift) % pair_i, 0, keepdims=False)
        arrived.append(lax.ppermute(sent, BOTH, route))
    stacked = jnp.stack(arrived)
    return jnp.stack(
        [
            lax.dynamic_index_in_dim(stacked, (col - slot) % pair_i, 0, keepdims=False)
            for slot in range(pair_i)
        ]
    )


def packed(pairs):
    width = pairs.shape[-1]
    total = jnp.swapaxes(pairs, 1, 2).astype(jnp.float32) + mirrored(pairs).astype(jnp.float32)
    d = lax.broadcasted_iota(jnp.int32, (width, width), 0)
    c = lax.broadcasted_iota(jnp.int32, (width, width), 1)
    weight = jnp.where(c < d, 1.0, jnp.where(c == d, 0.5, 0.0))
    total = (total * weight).astype(jnp.bfloat16)
    parts = []
    for low in range(0, width, GROUP):
        high = low + GROUP
        parts.append(total[:, low:high, :high].reshape(pairs.shape[0], GROUP * high))
    return jnp.concatenate(parts, axis=1)


def offsets(width):
    at = [0]
    for k in range(width // GROUP):
        at.append(at[-1] + GROUP * GROUP * (k + 1))
    return at


def load(start, rows, l_hbm, own, vectors, sems):
    blocks = vectors.shape[0] // GROUP
    copies = [pltpu.make_async_copy(l_hbm.at[pl.ds(start, rows)], own, sems.at[blocks])]
    for k in range(blocks):
        part = pl.ds(k * GROUP, GROUP)
        copies.append(pltpu.make_async_copy(l_hbm.at[part], vectors.at[part], sems.at[k]))
    for copy in copies:
        copy.start()
    return copies


def form(own, vectors, at, chunk, k, store):
    width, _, depth = vectors.shape
    high = GROUP * (k + 1)
    left = own[pl.ds(at * chunk, chunk), :high, :].reshape(chunk * high, depth)
    for pair in range(0, GROUP, 2):
        right = vectors[pl.ds(k * GROUP + pair, 2)].reshape(2 * width, depth)
        product = lax.dot_general(left, right, NT, preferred_element_type=jnp.float32)
        product = product.astype(jnp.bfloat16)
        for q in range(2):
            part = product[:, q * width : (q + 1) * width].reshape(chunk, high, width)
            store(pl.ds((pair + q) * high, high), part)


def tile_kernel(rows, chunk, start_ref, l_hbm, t_hbm, vectors, own, tile, sems, sent):
    width = vectors.shape[0]
    blocks = width // GROUP
    at_row = offsets(width)
    copies = load(start_ref[0], rows, l_hbm, own, vectors, sems)
    copies[0].wait()

    def out_copy(at, k):
        size = at_row[k + 1] - at_row[k]
        return pltpu.make_async_copy(
            tile.at[k % 2, :, pl.ds(0, size)],
            t_hbm.at[pl.ds(at * chunk, chunk), pl.ds(at_row[k], size)],
            sent.at[k % 2],
        )

    def step(at, carry):
        for k in range(blocks):
            pl.when(at == 0)(copies[k + 1].wait)
            if k >= 2:
                out_copy(at, k - 2).wait()
            else:
                pl.when(at > 0)(out_copy(at - 1, blocks - 2 + k).wait)

            def store(part, value, k=k):
                tile[k % 2, :, part] = value

            form(own, vectors, at, chunk, k, store)
            out_copy(at, k).start()
        return carry

    lax.fori_loop(0, rows // chunk, step, 0)
    last = rows // chunk - 1
    out_copy(last, blocks - 2).wait()
    out_copy(last, blocks - 1).wait()


def tiles(cholesky, start, rows):
    width, _, depth = cholesky.shape
    chunk = min(8, rows)
    size = offsets(width)[-1]
    return pl.pallas_call(
        functools.partial(tile_kernel, rows, chunk),
        out_shape=jax.ShapeDtypeStruct((rows, size, width), jnp.bfloat16),
        grid_spec=pltpu.PrefetchScalarGridSpec(
            num_scalar_prefetch=1,
            grid=(),
            in_specs=[ANY],
            out_specs=ANY,
            scratch_shapes=[
                pltpu.VMEM((width, width, depth), jnp.bfloat16),
                pltpu.VMEM((rows, width, depth), jnp.bfloat16),
                pltpu.VMEM((2, chunk, GROUP * width, width), jnp.bfloat16),
                pltpu.SemaphoreType.DMA((width // GROUP + 1,)),
                pltpu.SemaphoreType.DMA((2,)),
            ],
        ),
        compiler_params=pltpu.CompilerParams(vmem_limit_bytes=60 << 20),
        cost_estimate=pl.CostEstimate(
            flops=2 * rows * width * size * depth,
            bytes_accessed=2 * width * width * depth + 2 * rows * size * width,
            transcendentals=0,
        ),
    )(start, cholesky)


def ladder_kernel(
    early, chunk, start_ref, l_hbm, t_hbm, s_ref, out_ref, vectors, own, tile, ring, total, sems, got
):
    width = vectors.shape[0]
    blocks = width // GROUP
    late = own.shape[0]
    slots = ring.shape[0]
    at_row = offsets(width)
    copies = load(start_ref[0] + early, late, l_hbm, own, vectors, sems)

    def fetch(a):
        slot = lax.rem(a, slots)
        return pltpu.make_async_copy(t_hbm.at[a], ring.at[slot], got.at[slot])

    for a in range(slots):
        fetch(a).start()
    copies[0].wait()

    def step(at, carry):
        for k in range(blocks):
            pl.when(at == 0)(copies[k + 1].wait)

            def store(part, value):
                tile[:, part] = value

            form(own, vectors, at, chunk, k, store)
            weights = s_ref[:, at_row[k] : at_row[k + 1]]
            for a in range(chunk):
                value = lax.dot_general(
                    weights,
                    tile[a, : at_row[k + 1] - at_row[k], :],
                    NN,
                    preferred_element_type=jnp.float32,
                )
                if k == 0:
                    total[early + at * chunk + a] = value
                else:
                    total[early + at * chunk + a] += value
        return carry

    lax.fori_loop(0, late // chunk, step, 0)

    def rest(a, carry):
        fetch(a).wait()
        total[a] = lax.dot_general(
            s_ref[...], ring[lax.rem(a, slots)], NN, preferred_element_type=jnp.float32
        )
        pl.when(a + slots < early)(lambda: fetch(a + slots).start())
        return carry

    lax.fori_loop(0, early, rest, 0)
    out_ref[...] = jnp.swapaxes(total[...], 0, 1).astype(out_ref.dtype)


def ladder(cholesky, tile, weights, start, rows):
    width, _, depth = cholesky.shape
    early = tile.shape[0]
    late = rows - early
    pairs, size = weights.shape
    chunk = min(8, late)
    slots = min(early, 10)
    return pl.pallas_call(
        functools.partial(ladder_kernel, early, chunk),
        out_shape=jax.ShapeDtypeStruct((pairs, rows, width), jnp.bfloat16),
        grid_spec=pltpu.PrefetchScalarGridSpec(
            num_scalar_prefetch=1,
            grid=(),
            in_specs=[ANY, ANY, VMEM],
            out_specs=VMEM,
            scratch_shapes=[
                pltpu.VMEM((width, width, depth), jnp.bfloat16),
                pltpu.VMEM((late, width, depth), jnp.bfloat16),
                pltpu.VMEM((chunk, GROUP * width, width), jnp.bfloat16),
                pltpu.VMEM((slots, size, width), jnp.bfloat16),
                pltpu.VMEM((rows, pairs, width), jnp.float32),
                pltpu.SemaphoreType.DMA((width // GROUP + 1,)),
                pltpu.SemaphoreType.DMA((slots,)),
            ],
        ),
        compiler_params=pltpu.CompilerParams(vmem_limit_bytes=62 << 20),
        cost_estimate=pl.CostEstimate(
            flops=2 * width * size * (late * depth + rows * pairs),
            bytes_accessed=2 * width * width * depth + 2 * early * size * width,
            transcendentals=0,
        ),
    )(start, cholesky, tile, weights)


def collected(sums):
    count_i, count_j = lax.axis_size("pi"), lax.axis_size("pj")
    landed = lax.all_to_all(sums, BOTH, split_axis=0, concat_axis=0, tiled=True)
    landed = landed.reshape((count_i, count_j, -1) + landed.shape[1:]).astype(jnp.float32)
    return jnp.sum(landed, axis=1)


def shards(amplitudes, cholesky, other_terms):
    width = cholesky.shape[0]
    pair_i, pair_j = amplitudes.shape[:2]
    count_i, count_j = lax.axis_size("pi"), lax.axis_size("pj")
    devices = count_i * count_j
    assert pair_j == 1 and pair_i * count_i == count_j
    rows = width // count_i
    early = rows // 2
    start = (lax.axis_index("pi") * rows).reshape(1)
    own = packed(amplitudes.reshape(pair_i, width, width))
    copies = jnp.broadcast_to(own[None], (devices,) + own.shape).reshape(devices * pair_i, -1)
    weights = lax.all_to_all(copies, BOTH, split_axis=0, concat_axis=0, tiled=True)
    tile = tiles(cholesky, start, early)
    part = collected(ladder(cholesky, tile, weights, start, rows))
    part = jnp.swapaxes(part, 0, 1).reshape(pair_i, width, width)
    half = other_terms.reshape(pair_i, width, width) + 0.5 * part
    back = mirrored(half.astype(jnp.bfloat16))
    total = half + jnp.swapaxes(back, 1, 2).astype(jnp.float32)
    return total.reshape(other_terms.shape)


def solution(mesh):
    return jax.shard_map(
        shards,
        mesh=mesh,
        in_specs=(P("pi", "pj", None, None), P(None, None, "pj"), P("pi", "pj", None, None)),
        out_specs=P("pi", "pj", None, None),
        check_vma=False,
    )
```

```python
import functools

import jax
import jax.numpy as jnp
from jax import lax
from jax.experimental import pallas as pl
from jax.experimental.pallas import tpu as pltpu
from jax.sharding import PartitionSpec as P


BOTH = ("pi", "pj")
GROUP = 16
NT = (((1,), (1,)), ((), ()))
NN = (((1,), (0,)), ((), ()))
ANY = pl.BlockSpec(memory_space=pl.ANY)
VMEM = pl.BlockSpec(memory_space=pltpu.VMEM)


def mirrored(block):
    pair_i = block.shape[0]
    count_i, count_j = lax.axis_size("pi"), lax.axis_size("pj")
    col = lax.axis_index("pj")
    arrived = []
    for shift in range(pair_i):
        route = []
        for row in range(count_i):
            for at in range(count_j):
                to = (at // pair_i) * count_j + pair_i * row + (at + shift) % pair_i
                route.append((row * count_j + at, to))
        sent = lax.dynamic_index_in_dim(block, (col + shift) % pair_i, 0, keepdims=False)
        arrived.append(lax.ppermute(sent, BOTH, route))
    stacked = jnp.stack(arrived)
    return jnp.stack(
        [
            lax.dynamic_index_in_dim(stacked, (col - slot) % pair_i, 0, keepdims=False)
            for slot in range(pair_i)
        ]
    )


def packed(pairs):
    width = pairs.shape[-1]
    total = jnp.swapaxes(pairs, 1, 2).astype(jnp.float32) + mirrored(pairs).astype(jnp.float32)
    d = lax.broadcasted_iota(jnp.int32, (width, width), 0)
    c = lax.broadcasted_iota(jnp.int32, (width, width), 1)
    weight = jnp.where(c < d, 1.0, jnp.where(c == d, 0.5, 0.0))
    total = (total * weight).astype(jnp.bfloat16)
    parts = []
    for low in range(0, width, GROUP):
        high = low + GROUP
        parts.append(total[:, low:high, :high].reshape(pairs.shape[0], GROUP * high))
    return jnp.concatenate(parts, axis=1)


def offsets(width):
    at = [0]
    for k in range(width // GROUP):
        at.append(at[-1] + GROUP * GROUP * (k + 1))
    return at


AHEAD = 3


def loads(start, rows, l_hbm, own, vectors, sems):
    blocks = vectors.shape[0] // GROUP
    copies = [pltpu.make_async_copy(l_hbm.at[pl.ds(start, rows)], own, sems.at[blocks])]
    for k in range(blocks):
        part = pl.ds(k * GROUP, GROUP)
        copies.append(pltpu.make_async_copy(l_hbm.at[part], vectors.at[part], sems.at[k]))
    for copy in copies[: AHEAD + 1]:
        copy.start()
    copies[0].wait()
    return copies[1:]


def arrive(copies, k, then):
    copies[k].wait()
    if k + AHEAD < len(copies):
        copies[k + AHEAD].start()
    if k + 1 == len(copies):
        then()


def form(own, vectors, at, chunk, k, store):
    width, _, depth = vectors.shape
    high = GROUP * (k + 1)
    left = own[pl.ds(at * chunk, chunk), :high, :].reshape(chunk * high, depth)
    for pair in range(0, GROUP, 2):
        right = vectors[pl.ds(k * GROUP + pair, 2)].reshape(2 * width, depth)
        product = lax.dot_general(left, right, NT, preferred_element_type=jnp.float32)
        product = product.astype(jnp.bfloat16)
        for q in range(2):
            part = product[:, q * width : (q + 1) * width].reshape(chunk, high, width)
            store(pl.ds((pair + q) * high, high), part)


def tile_kernel(rows, chunk, start_ref, l_hbm, t_hbm, vectors, own, tile, sems, sent):
    width = vectors.shape[0]
    blocks = width // GROUP
    at_row = offsets(width)
    copies = loads(start_ref[0], rows, l_hbm, own, vectors, sems)

    def out_copy(at, k):
        size = at_row[k + 1] - at_row[k]
        return pltpu.make_async_copy(
            tile.at[k % 2, :, pl.ds(0, size)],
            t_hbm.at[pl.ds(at * chunk, chunk), pl.ds(at_row[k], size)],
            sent.at[k % 2],
        )

    def step(at, carry):
        for k in range(blocks):
            pl.when(at == 0)(functools.partial(arrive, copies, k, lambda: None))
            if k >= 2:
                out_copy(at, k - 2).wait()
            else:
                pl.when(at > 0)(out_copy(at - 1, blocks - 2 + k).wait)

            def store(part, value, k=k):
                tile[k % 2, :, part] = value

            form(own, vectors, at, chunk, k, store)
            out_copy(at, k).start()
        return carry

    lax.fori_loop(0, rows // chunk, step, 0)
    last = rows // chunk - 1
    out_copy(last, blocks - 2).wait()
    out_copy(last, blocks - 1).wait()


def tiles(cholesky, start, rows):
    width, _, depth = cholesky.shape
    chunk = min(8, rows)
    size = offsets(width)[-1]
    return pl.pallas_call(
        functools.partial(tile_kernel, rows, chunk),
        out_shape=jax.ShapeDtypeStruct((rows, size, width), jnp.bfloat16),
        grid_spec=pltpu.PrefetchScalarGridSpec(
            num_scalar_prefetch=1,
            grid=(),
            in_specs=[ANY],
            out_specs=ANY,
            scratch_shapes=[
                pltpu.VMEM((width, width, depth), jnp.bfloat16),
                pltpu.VMEM((rows, width, depth), jnp.bfloat16),
                pltpu.VMEM((2, chunk, GROUP * width, width), jnp.bfloat16),
                pltpu.SemaphoreType.DMA((width // GROUP + 1,)),
                pltpu.SemaphoreType.DMA((2,)),
            ],
        ),
        compiler_params=pltpu.CompilerParams(vmem_limit_bytes=60 << 20),
        cost_estimate=pl.CostEstimate(
            flops=2 * rows * width * size * depth,
            bytes_accessed=2 * width * width * depth + 2 * rows * size * width,
            transcendentals=0,
        ),
    )(start, cholesky)


def ladder_kernel(
    early, chunk, start_ref, l_hbm, t_hbm, s_ref, out_ref, vectors, own, tile, ring, total, sems, got
):
    width = vectors.shape[0]
    blocks = width // GROUP
    late = own.shape[0]
    slots = ring.shape[0]
    at_row = offsets(width)
    copies = loads(start_ref[0] + early, late, l_hbm, own, vectors, sems)

    def fetch(a):
        slot = lax.rem(a, slots)
        return pltpu.make_async_copy(t_hbm.at[a], ring.at[slot], got.at[slot])

    def prefetch():
        for a in range(slots):
            fetch(a).start()

    def step(at, carry):
        for k in range(blocks):
            pl.when(at == 0)(functools.partial(arrive, copies, k, prefetch))

            def store(part, value):
                tile[:, part] = value

            form(own, vectors, at, chunk, k, store)
            weights = s_ref[:, at_row[k] : at_row[k + 1]]
            for a in range(chunk):
                value = lax.dot_general(
                    weights,
                    tile[a, : at_row[k + 1] - at_row[k], :],
                    NN,
                    preferred_element_type=jnp.float32,
                )
                if k == 0:
                    total[early + at * chunk + a] = value
                else:
                    total[early + at * chunk + a] += value
        return carry

    lax.fori_loop(0, late // chunk, step, 0)

    def rest(a, carry):
        fetch(a).wait()
        total[a] = lax.dot_general(
            s_ref[...], ring[lax.rem(a, slots)], NN, preferred_element_type=jnp.float32
        )
        pl.when(a + slots < early)(lambda: fetch(a + slots).start())
        return carry

    lax.fori_loop(0, early, rest, 0)
    out_ref[...] = jnp.swapaxes(total[...], 0, 1).astype(out_ref.dtype)


def ladder(cholesky, tile, weights, start, rows):
    width, _, depth = cholesky.shape
    early = tile.shape[0]
    late = rows - early
    pairs, size = weights.shape
    chunk = min(8, late)
    slots = min(early, 10)
    return pl.pallas_call(
        functools.partial(ladder_kernel, early, chunk),
        out_shape=jax.ShapeDtypeStruct((pairs, rows, width), jnp.bfloat16),
        grid_spec=pltpu.PrefetchScalarGridSpec(
            num_scalar_prefetch=1,
            grid=(),
            in_specs=[ANY, ANY, VMEM],
            out_specs=VMEM,
            scratch_shapes=[
                pltpu.VMEM((width, width, depth), jnp.bfloat16),
                pltpu.VMEM((late, width, depth), jnp.bfloat16),
                pltpu.VMEM((chunk, GROUP * width, width), jnp.bfloat16),
                pltpu.VMEM((slots, size, width), jnp.bfloat16),
                pltpu.VMEM((rows, pairs, width), jnp.float32),
                pltpu.SemaphoreType.DMA((width // GROUP + 1,)),
                pltpu.SemaphoreType.DMA((slots,)),
            ],
        ),
        compiler_params=pltpu.CompilerParams(vmem_limit_bytes=62 << 20),
        cost_estimate=pl.CostEstimate(
            flops=2 * width * size * (late * depth + rows * pairs),
            bytes_accessed=2 * width * width * depth + 2 * early * size * width,
            transcendentals=0,
        ),
    )(start, cholesky, tile, weights)


def collected(sums):
    count_i, count_j = lax.axis_size("pi"), lax.axis_size("pj")
    landed = lax.all_to_all(sums, BOTH, split_axis=0, concat_axis=0, tiled=True)
    landed = landed.reshape((count_i, count_j, -1) + landed.shape[1:]).astype(jnp.float32)
    return jnp.sum(landed, axis=1)


def shards(amplitudes, cholesky, other_terms):
    width = cholesky.shape[0]
    pair_i, pair_j = amplitudes.shape[:2]
    count_i, count_j = lax.axis_size("pi"), lax.axis_size("pj")
    devices = count_i * count_j
    assert pair_j == 1 and pair_i * count_i == count_j
    rows = width // count_i
    early = rows // 2
    start = (lax.axis_index("pi") * rows).reshape(1)
    own = packed(amplitudes.reshape(pair_i, width, width))
    copies = jnp.broadcast_to(own[None], (devices,) + own.shape).reshape(devices * pair_i, -1)
    weights = lax.all_to_all(copies, BOTH, split_axis=0, concat_axis=0, tiled=True)
    tile = tiles(cholesky, start, early)
    part = collected(ladder(cholesky, tile, weights, start, rows))
    part = jnp.swapaxes(part, 0, 1).reshape(pair_i, width, width)
    half = other_terms.reshape(pair_i, width, width) + 0.5 * part
    back = mirrored(half.astype(jnp.bfloat16))
    total = half + jnp.swapaxes(back, 1, 2).astype(jnp.float32)
    return total.reshape(other_terms.shape)


def solution(mesh):
    return jax.shard_map(
        shards,
        mesh=mesh,
        in_specs=(P("pi", "pj", None, None), P(None, None, "pj"), P("pi", "pj", None, None)),
        out_specs=P("pi", "pj", None, None),
        check_vma=False,
    )
```

```python
import functools

import jax
import jax.numpy as jnp
from jax import lax
from jax.experimental import pallas as pl
from jax.experimental.pallas import tpu as pltpu
from jax.sharding import PartitionSpec as P


BOTH = ("pi", "pj")
GROUP = 16
NT = (((1,), (1,)), ((), ()))
NN = (((1,), (0,)), ((), ()))
ANY = pl.BlockSpec(memory_space=pl.ANY)
VMEM = pl.BlockSpec(memory_space=pltpu.VMEM)


def exchanged(block):
    pair_i = block.shape[0]
    count_i, count_j = lax.axis_size("pi"), lax.axis_size("pj")
    col = lax.axis_index("pj")
    arrived = []
    for shift in range(pair_i):
        route = []
        for row in range(count_i):
            for at in range(count_j):
                to = (at // pair_i) * count_j + pair_i * row + (at + shift) % pair_i
                route.append((row * count_j + at, to))
        sent = lax.dynamic_index_in_dim(block, (col + shift) % pair_i, 0, keepdims=False)
        arrived.append(lax.ppermute(sent, BOTH, route))
    return arrived


def mirrored(block):
    pair_i = block.shape[0]
    stacked = jnp.stack(exchanged(block))
    col = lax.axis_index("pj")
    return jnp.stack(
        [
            lax.dynamic_index_in_dim(stacked, (col - slot) % pair_i, 0, keepdims=False)
            for slot in range(pair_i)
        ]
    )


def groups(width):
    blocks = width // GROUP
    middle = (blocks - 2) // 2
    return [(k, blocks - 2 - k) for k in range(middle)] + [(middle,), (blocks - 1,)]


def group_rows(width):
    at = [0]
    for group in groups(width):
        at.append(at[-1] + GROUP * GROUP * sum(k + 1 for k in group) // width)
    return at


def place(width, group, k, d):
    high = GROUP * (k + 1)
    if len(group) == 2:
        return d * width + (0 if k == group[0] else width - high)
    wrap = GROUP * high // width
    return d % wrap * width + d // wrap * high


def pack_kernel(col_ref, own_ref, *refs):
    pair_i, width, _ = own_ref.shape
    arrived, out_ref, packed = refs[:pair_i], refs[pair_i], refs[pair_i + 1]
    d = lax.broadcasted_iota(jnp.int32, (width, width), 0)
    c = lax.broadcasted_iota(jnp.int32, (width, width), 1)
    weight = jnp.where(c < d, 1.0, jnp.where(c == d, 0.5, 0.0)).astype(jnp.float32)
    rows = group_rows(width)
    for slot in range(pair_i):
        which = lax.rem(col_ref[0] - slot + pair_i, pair_i)
        back = arrived[0][...].astype(jnp.float32)
        for m in range(1, pair_i):
            back = jnp.where(which == m, arrived[m][...].astype(jnp.float32), back)
        total = (jnp.swapaxes(own_ref[slot].astype(jnp.float32), 0, 1) + back) * weight
        for g, group in enumerate(groups(width)):
            lines = rows[g + 1] - rows[g]
            value = 0.0
            for k in group:
                for first in range(0, GROUP, lines):
                    low = place(width, group, k, first)
                    part = total[GROUP * k + first : GROUP * k + first + lines]
                    value = value + (pltpu.roll(part, low, 1) if low else part)
            packed[slot, rows[g] : rows[g + 1]] = value
    final = packed[...].astype(jnp.bfloat16)

    def copy(at, carry):
        out_ref[at] = final
        return carry

    lax.fori_loop(0, out_ref.shape[0], copy, 0)


def packed_copies(pairs, devices):
    pair_i, width, _ = pairs.shape
    lines = group_rows(width)[-1]
    arrived = exchanged(pairs)
    return pl.pallas_call(
        pack_kernel,
        out_shape=jax.ShapeDtypeStruct((devices, pair_i, lines, width), jnp.bfloat16),
        in_specs=[pl.BlockSpec(memory_space=pltpu.SMEM)] + [VMEM] * (1 + pair_i),
        out_specs=VMEM,
        scratch_shapes=[pltpu.VMEM((pair_i, lines, width), jnp.float32)],
        compiler_params=pltpu.CompilerParams(vmem_limit_bytes=40 << 20),
    )(lax.axis_index("pj").reshape(1), pairs, *arrived)


AHEAD = 3


def loads(start, rows, l_hbm, own, vectors, sems):
    width = vectors.shape[0]
    first = pltpu.make_async_copy(l_hbm.at[pl.ds(start, rows)], own, sems.at[width // GROUP])
    copies = []
    for k in [k for group in groups(width) for k in group]:
        part = pl.ds(k * GROUP, GROUP)
        copies.append(pltpu.make_async_copy(l_hbm.at[part], vectors.at[part], sems.at[k]))
    first.start()
    for copy in copies[:AHEAD]:
        copy.start()
    first.wait()
    return copies


def arrive(copies, n):
    copies[n].wait()
    if n + AHEAD < len(copies):
        copies[n + AHEAD].start()


def form(own, vectors, tile, group, k):
    rows, width, depth = own.shape
    high = GROUP * (k + 1)
    chunk = min(16 if 2 * high <= width else 8, rows)

    def step(at, carry):
        if chunk == rows:
            left = own[:, :high, :]
            part = slice(None)
        else:
            part = pl.ds(pl.multiple_of(at * chunk, chunk), chunk)
            left = own[part, :high, :]
        left = left.reshape(chunk * high, depth)
        for d in range(0, GROUP, 2):
            right = vectors[pl.ds(k * GROUP + d, 2)].reshape(2 * width, depth)
            product = lax.dot_general(left, right, NT, preferred_element_type=jnp.float32)
            product = product.astype(jnp.bfloat16)
            for q in range(2):
                value = product[:, q * width : (q + 1) * width].reshape(chunk, high, width)
                tile[part, pl.ds(place(width, group, k, d + q), high)] = value
        return carry

    if chunk == rows:
        step(0, 0)
    else:
        lax.fori_loop(0, rows // chunk, step, 0)


def tile_kernel(start_ref, l_hbm, t_hbm, vectors, own, tile, sems, sent):
    rows, width, _ = own.shape
    lines = group_rows(width)
    copies = loads(start_ref[0], rows, l_hbm, own, vectors, sems)
    n = 0
    outs = []
    for g, group in enumerate(groups(width)):
        if g >= 2:
            outs[g - 2].wait()
        for k in group:
            arrive(copies, n)
            n += 1
            form(own, vectors, tile.at[g % 2], group, k)
        low, size = lines[g] * width, (lines[g + 1] - lines[g]) * width
        outs.append(
            pltpu.make_async_copy(
                tile.at[g % 2, :, pl.ds(0, size)], t_hbm.at[:, pl.ds(low, size)], sent.at[g % 2]
            )
        )
        outs[g].start()
    for copy in outs[-2:]:
        copy.wait()


def tiles(cholesky, start, rows):
    width, _, depth = cholesky.shape
    size = group_rows(width)[-1] * width
    return pl.pallas_call(
        tile_kernel,
        out_shape=jax.ShapeDtypeStruct((rows, size, width), jnp.bfloat16),
        grid_spec=pltpu.PrefetchScalarGridSpec(
            num_scalar_prefetch=1,
            grid=(),
            in_specs=[ANY],
            out_specs=ANY,
            scratch_shapes=[
                pltpu.VMEM((width, width, depth), jnp.bfloat16),
                pltpu.VMEM((rows, width, depth), jnp.bfloat16),
                pltpu.VMEM((2, rows, GROUP * width, width), jnp.bfloat16),
                pltpu.SemaphoreType.DMA((width // GROUP + 1,)),
                pltpu.SemaphoreType.DMA((2,)),
            ],
        ),
        compiler_params=pltpu.CompilerParams(vmem_limit_bytes=60 << 20),
        cost_estimate=pl.CostEstimate(
            flops=2 * rows * width * size * depth,
            bytes_accessed=2 * width * width * depth + 2 * rows * size * width,
            transcendentals=0,
        ),
    )(start, cholesky)


def ladder_kernel(
    early, start_ref, l_hbm, t_hbm, s_ref, out_ref, vectors, own, tile, ring, total, sems, got
):
    late, width, _ = own.shape
    slots = ring.shape[0]
    lines = group_rows(width)
    copies = loads(start_ref[0] + early, late, l_hbm, own, vectors, sems)

    def fetch(a):
        slot = lax.rem(a, slots)
        return pltpu.make_async_copy(t_hbm.at[a], ring.at[slot], got.at[slot])

    n = 0
    for g, group in enumerate(groups(width)):
        for k in group:
            arrive(copies, n)
            n += 1
            if n == len(copies):
                for a in range(slots):
                    fetch(a).start()
            form(own, vectors, tile, group, k)
        size = (lines[g + 1] - lines[g]) * width
        weights = s_ref[:, lines[g] * width : lines[g + 1] * width]
        batch = min(8, late)

        def apply(at, carry, g=g, size=size, weights=weights):
            for q in range(0, batch, 2):
                a = at * batch + q
                both = jnp.concatenate([tile[a, :size], tile[a + 1, :size]], axis=1)
                value = lax.dot_general(weights, both, NN, preferred_element_type=jnp.float32)
                for h in range(2):
                    part = value[:, h * width : (h + 1) * width]
                    if g == 0:
                        total[early + a + h] = part
                    else:
                        total[early + a + h] += part
            return carry

        lax.fori_loop(0, late // batch, apply, 0)

    def rest(at, carry):
        a = 2 * at
        fetch(a).wait()
        fetch(a + 1).wait()
        both = jnp.concatenate([ring[lax.rem(a, slots)], ring[lax.rem(a + 1, slots)]], axis=1)
        value = lax.dot_general(s_ref[...], both, NN, preferred_element_type=jnp.float32)
        total[a] = value[:, :width]
        total[a + 1] = value[:, width:]
        pl.when(a + slots < early)(lambda: fetch(a + slots).start())
        pl.when(a + 1 + slots < early)(lambda: fetch(a + 1 + slots).start())
        return carry

    lax.fori_loop(0, early // 2, rest, 0)
    out_ref[...] = jnp.swapaxes(total[...], 0, 1).astype(out_ref.dtype)


def ladder(cholesky, tile, weights, start, rows):
    width, _, depth = cholesky.shape
    early = tile.shape[0]
    late = rows - early
    pairs, size = weights.shape
    slots = min(early, 8)
    return pl.pallas_call(
        functools.partial(ladder_kernel, early),
        out_shape=jax.ShapeDtypeStruct((pairs, rows, width), jnp.bfloat16),
        grid_spec=pltpu.PrefetchScalarGridSpec(
            num_scalar_prefetch=1,
            grid=(),
            in_specs=[ANY, ANY, VMEM],
            out_specs=VMEM,
            scratch_shapes=[
                pltpu.VMEM((width, width, depth), jnp.bfloat16),
                pltpu.VMEM((late, width, depth), jnp.bfloat16),
                pltpu.VMEM((late, GROUP * width, width), jnp.bfloat16),
                pltpu.VMEM((slots, size, width), jnp.bfloat16),
                pltpu.VMEM((rows, pairs, width), jnp.float32),
                pltpu.SemaphoreType.DMA((width // GROUP + 1,)),
                pltpu.SemaphoreType.DMA((slots,)),
            ],
        ),
        compiler_params=pltpu.CompilerParams(vmem_limit_bytes=62 << 20),
        cost_estimate=pl.CostEstimate(
            flops=2 * width * size * (late * depth + rows * pairs),
            bytes_accessed=2 * width * width * depth + 2 * early * size * width,
            transcendentals=0,
        ),
    )(start, cholesky, tile, weights)


def collected(sums):
    count_i, count_j = lax.axis_size("pi"), lax.axis_size("pj")
    landed = lax.all_to_all(sums, BOTH, split_axis=0, concat_axis=0, tiled=True)
    landed = landed.reshape((count_i, count_j, -1) + landed.shape[1:]).astype(jnp.float32)
    return jnp.sum(landed, axis=1)


def shards(amplitudes, cholesky, other_terms):
    width = cholesky.shape[0]
    pair_i, pair_j = amplitudes.shape[:2]
    count_i, count_j = lax.axis_size("pi"), lax.axis_size("pj")
    devices = count_i * count_j
    assert pair_j == 1 and pair_i * count_i == count_j
    rows = width // count_i
    early = rows // 2
    start = (lax.axis_index("pi") * rows).reshape(1)
    copies = packed_copies(amplitudes.reshape(pair_i, width, width), devices)
    weights = lax.all_to_all(copies, BOTH, split_axis=0, concat_axis=0, tiled=True)
    weights = weights.reshape(devices * pair_i, -1)
    tile = tiles(cholesky, start, early)
    part = collected(ladder(cholesky, tile, weights, start, rows))
    part = jnp.swapaxes(part, 0, 1).reshape(pair_i, width, width)
    half = other_terms.reshape(pair_i, width, width) + 0.5 * part
    back = mirrored(half.astype(jnp.bfloat16))
    total = half + jnp.swapaxes(back, 1, 2).astype(jnp.float32)
    return total.reshape(other_terms.shape)


def solution(mesh):
    return jax.shard_map(
        shards,
        mesh=mesh,
        in_specs=(P("pi", "pj", None, None), P(None, None, "pj"), P("pi", "pj", None, None)),
        out_specs=P("pi", "pj", None, None),
        check_vma=False,
    )
```

```python
import functools

import jax
import jax.numpy as jnp
from jax import lax
from jax.experimental import pallas as pl
from jax.experimental.pallas import tpu as pltpu
from jax.sharding import PartitionSpec as P


BOTH = ("pi", "pj")
GROUP = 16
NT = (((1,), (1,)), ((), ()))
NN = (((1,), (0,)), ((), ()))
ANY = pl.BlockSpec(memory_space=pl.ANY)
VMEM = pl.BlockSpec(memory_space=pltpu.VMEM)


def exchanged(block):
    pair_i = block.shape[0]
    count_i, count_j = lax.axis_size("pi"), lax.axis_size("pj")
    col = lax.axis_index("pj")
    arrived = []
    for shift in range(pair_i):
        route = []
        for row in range(count_i):
            for at in range(count_j):
                to = (at // pair_i) * count_j + pair_i * row + (at + shift) % pair_i
                route.append((row * count_j + at, to))
        sent = lax.dynamic_index_in_dim(block, (col + shift) % pair_i, 0, keepdims=False)
        arrived.append(lax.ppermute(sent, BOTH, route))
    return arrived


def mirrored(block):
    pair_i = block.shape[0]
    stacked = jnp.stack(exchanged(block))
    col = lax.axis_index("pj")
    return jnp.stack(
        [
            lax.dynamic_index_in_dim(stacked, (col - slot) % pair_i, 0, keepdims=False)
            for slot in range(pair_i)
        ]
    )


def groups(width):
    blocks = width // GROUP
    middle = (blocks - 2) // 2
    return [(k, blocks - 2 - k) for k in range(middle)] + [(middle,), (blocks - 1,)]


def group_rows(width):
    at = [0]
    for group in groups(width):
        at.append(at[-1] + GROUP * GROUP * sum(k + 1 for k in group) // width)
    return at


def place(width, group, k, d):
    high = GROUP * (k + 1)
    if len(group) == 2:
        return d * width + (0 if k == group[0] else width - high)
    wrap = GROUP * high // width
    return d % wrap * width + d // wrap * high


def pack_kernel(col_ref, own_ref, *refs):
    pair_i, width, _ = own_ref.shape
    arrived, out_ref, packed = refs[:pair_i], refs[pair_i], refs[pair_i + 1]
    d = lax.broadcasted_iota(jnp.int32, (width, width), 0)
    c = lax.broadcasted_iota(jnp.int32, (width, width), 1)
    weight = jnp.where(c < d, 1.0, jnp.where(c == d, 0.5, 0.0)).astype(jnp.float32)
    rows = group_rows(width)
    for slot in range(pair_i):
        which = lax.rem(col_ref[0] - slot + pair_i, pair_i)
        back = arrived[0][...].astype(jnp.float32)
        for m in range(1, pair_i):
            back = jnp.where(which == m, arrived[m][...].astype(jnp.float32), back)
        total = (jnp.swapaxes(own_ref[slot].astype(jnp.float32), 0, 1) + back) * weight
        for g, group in enumerate(groups(width)):
            lines = rows[g + 1] - rows[g]
            value = 0.0
            for k in group:
                for first in range(0, GROUP, lines):
                    low = place(width, group, k, first)
                    part = total[GROUP * k + first : GROUP * k + first + lines]
                    value = value + (pltpu.roll(part, low, 1) if low else part)
            packed[slot, rows[g] : rows[g + 1]] = value
    final = packed[...].astype(jnp.bfloat16)

    def copy(at, carry):
        out_ref[at] = final
        return carry

    lax.fori_loop(0, out_ref.shape[0], copy, 0)


def packed_copies(pairs, devices):
    pair_i, width, _ = pairs.shape
    lines = group_rows(width)[-1]
    arrived = exchanged(pairs)
    return pl.pallas_call(
        pack_kernel,
        out_shape=jax.ShapeDtypeStruct((devices, pair_i, lines, width), jnp.bfloat16),
        in_specs=[pl.BlockSpec(memory_space=pltpu.SMEM)] + [VMEM] * (1 + pair_i),
        out_specs=VMEM,
        scratch_shapes=[pltpu.VMEM((pair_i, lines, width), jnp.float32)],
        compiler_params=pltpu.CompilerParams(vmem_limit_bytes=40 << 20),
    )(lax.axis_index("pj").reshape(1), pairs, *arrived)


AHEAD = 3


def loads(start, rows, l_hbm, own, vectors, sems):
    width = vectors.shape[0]
    first = pltpu.make_async_copy(l_hbm.at[pl.ds(start, rows)], own, sems.at[width // GROUP])
    copies = []
    for k in [k for group in groups(width) for k in group]:
        part = pl.ds(k * GROUP, GROUP)
        copies.append(pltpu.make_async_copy(l_hbm.at[part], vectors.at[part], sems.at[k]))
    first.start()
    for copy in copies[:AHEAD]:
        copy.start()
    first.wait()
    return copies


def arrive(copies, n):
    copies[n].wait()
    if n + AHEAD < len(copies):
        copies[n + AHEAD].start()


def form(own, vectors, tile, group, k, most):
    rows, width, depth = own.shape
    high = GROUP * (k + 1)
    chunk = min(16 if 2 * high <= width else most, rows)

    def step(at, carry):
        if chunk == rows:
            left = own[:, :high, :]
            part = slice(None)
        else:
            part = pl.ds(pl.multiple_of(at * chunk, chunk), chunk)
            left = own[part, :high, :]
        left = left.reshape(chunk * high, depth)
        for d in range(0, GROUP, 2):
            right = vectors[pl.ds(k * GROUP + d, 2)].reshape(2 * width, depth)
            product = lax.dot_general(left, right, NT, preferred_element_type=jnp.float32)
            product = product.astype(jnp.bfloat16)
            for q in range(2):
                value = product[:, q * width : (q + 1) * width].reshape(chunk, high, width)
                tile[part, pl.ds(place(width, group, k, d + q), high)] = value
        return carry

    if chunk == rows:
        step(0, 0)
    else:
        lax.fori_loop(0, rows // chunk, step, 0)


def tile_kernel(start_ref, l_hbm, t_hbm, vectors, own, tile, sems, sent):
    rows, width, _ = own.shape
    lines = group_rows(width)
    copies = loads(start_ref[0], rows, l_hbm, own, vectors, sems)
    n = 0
    outs = []
    for g, group in enumerate(groups(width)):
        if g >= 2:
            outs[g - 2].wait()
        for k in group:
            arrive(copies, n)
            n += 1
            form(own, vectors, tile.at[g % 2], group, k, 8)
        low, size = lines[g] * width, (lines[g + 1] - lines[g]) * width
        outs.append(
            pltpu.make_async_copy(
                tile.at[g % 2, :, pl.ds(0, size)], t_hbm.at[:, pl.ds(low, size)], sent.at[g % 2]
            )
        )
        outs[g].start()
    for copy in outs[-2:]:
        copy.wait()


def tiles(cholesky, start, rows):
    width, _, depth = cholesky.shape
    size = group_rows(width)[-1] * width
    return pl.pallas_call(
        tile_kernel,
        out_shape=jax.ShapeDtypeStruct((rows, size, width), jnp.bfloat16),
        grid_spec=pltpu.PrefetchScalarGridSpec(
            num_scalar_prefetch=1,
            grid=(),
            in_specs=[ANY],
            out_specs=ANY,
            scratch_shapes=[
                pltpu.VMEM((width, width, depth), jnp.bfloat16),
                pltpu.VMEM((rows, width, depth), jnp.bfloat16),
                pltpu.VMEM((2, rows, GROUP * width, width), jnp.bfloat16),
                pltpu.SemaphoreType.DMA((width // GROUP + 1,)),
                pltpu.SemaphoreType.DMA((2,)),
            ],
        ),
        compiler_params=pltpu.CompilerParams(vmem_limit_bytes=60 << 20),
        cost_estimate=pl.CostEstimate(
            flops=2 * rows * width * size * depth,
            bytes_accessed=2 * width * width * depth + 2 * rows * size * width,
            transcendentals=0,
        ),
    )(start, cholesky)


def ladder_kernel(
    early, start_ref, l_hbm, t_hbm, s_ref, out_ref, vectors, own, tile, ring, total, sems, got
):
    late, width, _ = own.shape
    slots = ring.shape[0]
    lines = group_rows(width)
    copies = loads(start_ref[0] + early, late, l_hbm, own, vectors, sems)

    def fetch(a):
        slot = lax.rem(a, slots)
        return pltpu.make_async_copy(t_hbm.at[a], ring.at[slot], got.at[slot])

    n = 0
    for g, group in enumerate(groups(width)):
        for k in group:
            arrive(copies, n)
            n += 1
            if n == len(copies):
                for a in range(slots):
                    fetch(a).start()
            form(own, vectors, tile, group, k, 16)
        size = (lines[g + 1] - lines[g]) * width
        weights = s_ref[:, lines[g] * width : lines[g + 1] * width]
        batch = min(16, late)

        def apply(at, carry, g=g, size=size, weights=weights):
            for q in range(batch):
                a = at * batch + q
                value = lax.dot_general(
                    weights, tile[a, :size], NN, preferred_element_type=jnp.float32
                )
                if g == 0:
                    total[early + a] = value
                else:
                    total[early + a] += value
            return carry

        lax.fori_loop(0, late // batch, apply, 0)

    def rest(at, carry):
        a = 2 * at
        fetch(a).wait()
        fetch(a + 1).wait()
        both = jnp.concatenate([ring[lax.rem(a, slots)], ring[lax.rem(a + 1, slots)]], axis=1)
        value = lax.dot_general(s_ref[...], both, NN, preferred_element_type=jnp.float32)
        total[a] = value[:, :width]
        total[a + 1] = value[:, width:]
        pl.when(a + slots < early)(lambda: fetch(a + slots).start())
        pl.when(a + 1 + slots < early)(lambda: fetch(a + 1 + slots).start())
        return carry

    lax.fori_loop(0, early // 2, rest, 0)
    out_ref[...] = jnp.swapaxes(total[...], 0, 1).astype(out_ref.dtype)


def ladder(cholesky, tile, weights, start, rows):
    width, _, depth = cholesky.shape
    early = tile.shape[0]
    late = rows - early
    pairs, size = weights.shape
    slots = min(early, 8)
    return pl.pallas_call(
        functools.partial(ladder_kernel, early),
        out_shape=jax.ShapeDtypeStruct((pairs, rows, width), jnp.bfloat16),
        grid_spec=pltpu.PrefetchScalarGridSpec(
            num_scalar_prefetch=1,
            grid=(),
            in_specs=[ANY, ANY, VMEM],
            out_specs=VMEM,
            scratch_shapes=[
                pltpu.VMEM((width, width, depth), jnp.bfloat16),
                pltpu.VMEM((late, width, depth), jnp.bfloat16),
                pltpu.VMEM((late, GROUP * width, width), jnp.bfloat16),
                pltpu.VMEM((slots, size, width), jnp.bfloat16),
                pltpu.VMEM((rows, pairs, width), jnp.float32),
                pltpu.SemaphoreType.DMA((width // GROUP + 1,)),
                pltpu.SemaphoreType.DMA((slots,)),
            ],
        ),
        compiler_params=pltpu.CompilerParams(vmem_limit_bytes=62 << 20),
        cost_estimate=pl.CostEstimate(
            flops=2 * width * size * (late * depth + rows * pairs),
            bytes_accessed=2 * width * width * depth + 2 * early * size * width,
            transcendentals=0,
        ),
    )(start, cholesky, tile, weights)


def collected(sums):
    count_i, count_j = lax.axis_size("pi"), lax.axis_size("pj")
    landed = lax.all_to_all(sums, BOTH, split_axis=0, concat_axis=0, tiled=True)
    landed = landed.reshape((count_i, count_j, -1) + landed.shape[1:]).astype(jnp.float32)
    return jnp.sum(landed, axis=1)


def shards(amplitudes, cholesky, other_terms):
    width = cholesky.shape[0]
    pair_i, pair_j = amplitudes.shape[:2]
    count_i, count_j = lax.axis_size("pi"), lax.axis_size("pj")
    devices = count_i * count_j
    assert pair_j == 1 and pair_i * count_i == count_j
    rows = width // count_i
    early = rows // 2
    start = (lax.axis_index("pi") * rows).reshape(1)
    copies = packed_copies(amplitudes.reshape(pair_i, width, width), devices)
    weights = lax.all_to_all(copies, BOTH, split_axis=0, concat_axis=0, tiled=True)
    weights = weights.reshape(devices * pair_i, -1)
    tile = tiles(cholesky, start, early)
    part = collected(ladder(cholesky, tile, weights, start, rows))
    part = jnp.swapaxes(part, 0, 1).reshape(pair_i, width, width)
    half = other_terms.reshape(pair_i, width, width) + 0.5 * part
    back = mirrored(half.astype(jnp.bfloat16))
    total = half + jnp.swapaxes(back, 1, 2).astype(jnp.float32)
    return total.reshape(other_terms.shape)


def solution(mesh):
    return jax.shard_map(
        shards,
        mesh=mesh,
        in_specs=(P("pi", "pj", None, None), P(None, None, "pj"), P("pi", "pj", None, None)),
        out_specs=P("pi", "pj", None, None),
        check_vma=False,
    )
```

```python
import functools

import jax
import jax.numpy as jnp
from jax import lax
from jax.experimental import pallas as pl
from jax.experimental.pallas import tpu as pltpu
from jax.sharding import PartitionSpec as P


BOTH = ("pi", "pj")
GROUP = 16
NT = (((1,), (1,)), ((), ()))
NN = (((1,), (0,)), ((), ()))
ANY = pl.BlockSpec(memory_space=pl.ANY)
VMEM = pl.BlockSpec(memory_space=pltpu.VMEM)


def exchanged(block):
    pair_i = block.shape[0]
    count_i, count_j = lax.axis_size("pi"), lax.axis_size("pj")
    col = lax.axis_index("pj")
    own, arrived = [], []
    for shift in range(pair_i):
        route = []
        for row in range(count_i):
            for at in range(count_j):
                to = (at // pair_i) * count_j + pair_i * row + (at + shift) % pair_i
                route.append((row * count_j + at, to))
        sent = lax.dynamic_index_in_dim(block, (col + shift) % pair_i, 0, keepdims=False)
        own.append(sent)
        arrived.append(lax.ppermute(sent, BOTH, route))
    return own, arrived


def mirrored(block):
    pair_i = block.shape[0]
    stacked = jnp.stack(exchanged(block)[1])
    col = lax.axis_index("pj")
    return jnp.stack(
        [
            lax.dynamic_index_in_dim(stacked, (col - slot) % pair_i, 0, keepdims=False)
            for slot in range(pair_i)
        ]
    )


def groups(width):
    blocks = width // GROUP
    middle = (blocks - 2) // 2
    return [(blocks - 1,)] + [(k, blocks - 2 - k) for k in range(middle)] + [(middle,)]


def group_rows(width):
    at = [0]
    for group in groups(width):
        at.append(at[-1] + GROUP * GROUP * sum(k + 1 for k in group) // width)
    return at


def place(width, group, k, d):
    high = GROUP * (k + 1)
    if len(group) == 2:
        return d * width + (0 if k == group[0] else width - high)
    wrap = GROUP * high // width
    return d % wrap * width + d // wrap * high


def chosen(refs, which):
    value = refs[0][...].astype(jnp.float32)
    for m in range(1, len(refs)):
        value = jnp.where(which == m, refs[m][...].astype(jnp.float32), value)
    return value


def pack_kernel(pair_i, col_ref, *refs):
    own, arrived = refs[:pair_i], refs[pair_i : 2 * pair_i]
    out_ref, packed = refs[2 * pair_i :]
    width = own[0].shape[0]
    turn = lax.rem(col_ref[0], pair_i)
    d = lax.broadcasted_iota(jnp.int32, (width, width), 0)
    c = lax.broadcasted_iota(jnp.int32, (width, width), 1)
    weight = jnp.where(c < d, 1.0, jnp.where(c == d, 0.5, 0.0)).astype(jnp.float32)
    rows = group_rows(width)
    for slot in range(pair_i):
        mine = chosen(own, lax.rem(slot - turn + pair_i, pair_i))
        back = chosen(arrived, lax.rem(turn - slot + pair_i, pair_i))
        total = (jnp.swapaxes(mine, 0, 1) + back) * weight
        for g, group in enumerate(groups(width)):
            lines = rows[g + 1] - rows[g]
            value = 0.0
            for k in group:
                for first in range(0, GROUP, lines):
                    low = place(width, group, k, first)
                    part = total[GROUP * k + first : GROUP * k + first + lines]
                    value = value + (pltpu.roll(part, low, 1) if low else part)
            packed[slot, rows[g] : rows[g + 1]] = value
    final = packed[...].astype(jnp.bfloat16)

    def copy(at, carry):
        out_ref[at] = final
        return carry

    lax.fori_loop(0, out_ref.shape[0], copy, 0)


def packed_copies(pairs, devices):
    pair_i, width, _ = pairs.shape
    lines = group_rows(width)[-1]
    own, arrived = exchanged(pairs)
    return pl.pallas_call(
        functools.partial(pack_kernel, pair_i),
        out_shape=jax.ShapeDtypeStruct((devices, pair_i, lines, width), jnp.bfloat16),
        in_specs=[pl.BlockSpec(memory_space=pltpu.SMEM)] + [VMEM] * (2 * pair_i),
        out_specs=VMEM,
        scratch_shapes=[pltpu.VMEM((pair_i, lines, width), jnp.float32)],
        compiler_params=pltpu.CompilerParams(vmem_limit_bytes=40 << 20),
    )(lax.axis_index("pj").reshape(1), *own, *arrived)


AHEAD = 3


def loads(start, rows, l_hbm, own, vectors, sems, order):
    width = vectors.shape[0]
    first = pltpu.make_async_copy(l_hbm.at[pl.ds(start, rows)], own, sems.at[width // GROUP])
    copies = []
    for k in [k for group in order for k in group]:
        part = pl.ds(k * GROUP, GROUP)
        copies.append(pltpu.make_async_copy(l_hbm.at[part], vectors.at[part], sems.at[k]))
    first.start()
    for copy in copies[:2]:
        copy.start()
    first.wait()
    return copies


def arrive(copies, n):
    copies[n].wait()
    for copy in copies[2 : 1 + AHEAD] if n == 0 else copies[n + AHEAD : n + AHEAD + 1]:
        copy.start()


def form(own, vectors, tile, group, k, most):
    rows, width, depth = own.shape
    high = GROUP * (k + 1)
    chunk = min(16 if 2 * high <= width else most, rows)

    def step(at, carry):
        if chunk == rows:
            left = own[:, :high, :]
            part = slice(None)
        else:
            part = pl.ds(pl.multiple_of(at * chunk, chunk), chunk)
            left = own[part, :high, :]
        left = left.reshape(chunk * high, depth)
        for d in range(0, GROUP, 2):
            right = vectors[pl.ds(k * GROUP + d, 2)].reshape(2 * width, depth)
            product = lax.dot_general(left, right, NT, preferred_element_type=jnp.float32)
            product = product.astype(jnp.bfloat16)
            for q in range(2):
                value = product[:, q * width : (q + 1) * width].reshape(chunk, high, width)
                tile[part, pl.ds(place(width, group, k, d + q), high)] = value
        return carry

    if chunk == rows:
        step(0, 0)
    else:
        lax.fori_loop(0, rows // chunk, step, 0)


def tile_kernel(start_ref, l_hbm, t_hbm, vectors, own, tile, sems, sent):
    rows, width, _ = own.shape
    lines = group_rows(width)
    copies = loads(start_ref[0], rows, l_hbm, own, vectors, sems, groups(width))
    n = 0
    outs = []
    for g, group in enumerate(groups(width)):
        if g >= 2:
            outs[g - 2].wait()
        for k in group:
            arrive(copies, n)
            n += 1
            form(own, vectors, tile.at[g % 2], group, k, 8)
        low, size = lines[g] * width, (lines[g + 1] - lines[g]) * width
        outs.append(
            pltpu.make_async_copy(
                tile.at[g % 2, :, pl.ds(0, size)], t_hbm.at[:, pl.ds(low, size)], sent.at[g % 2]
            )
        )
        outs[g].start()
    for copy in outs[-2:]:
        copy.wait()


def tiles(cholesky, start, rows):
    width, _, depth = cholesky.shape
    size = group_rows(width)[-1] * width
    return pl.pallas_call(
        tile_kernel,
        out_shape=jax.ShapeDtypeStruct((rows, size, width), jnp.bfloat16),
        grid_spec=pltpu.PrefetchScalarGridSpec(
            num_scalar_prefetch=1,
            grid=(),
            in_specs=[ANY],
            out_specs=ANY,
            scratch_shapes=[
                pltpu.VMEM((width, width, depth), jnp.bfloat16),
                pltpu.VMEM((rows, width, depth), jnp.bfloat16),
                pltpu.VMEM((2, rows, GROUP * width, width), jnp.bfloat16),
                pltpu.SemaphoreType.DMA((width // GROUP + 1,)),
                pltpu.SemaphoreType.DMA((2,)),
            ],
        ),
        compiler_params=pltpu.CompilerParams(vmem_limit_bytes=60 << 20),
        cost_estimate=pl.CostEstimate(
            flops=2 * rows * width * size * depth,
            bytes_accessed=2 * width * width * depth + 2 * rows * size * width,
            transcendentals=0,
        ),
    )(start, cholesky)


def ladder_kernel(
    early, start_ref, l_hbm, t_hbm, s_ref, out_ref, vectors, own, tile, ring, total, sems, got
):
    late, width, _ = own.shape
    slots = ring.shape[0]
    lines = group_rows(width)
    order = groups(width)
    order = order[1:] + order[:1]
    copies = loads(start_ref[0] + early, late, l_hbm, own, vectors, sems, order)

    def fetch(a):
        slot = lax.rem(a, slots)
        return pltpu.make_async_copy(t_hbm.at[a], ring.at[slot], got.at[slot])

    n = 0
    for group in order:
        g = groups(width).index(group)
        for k in group:
            arrive(copies, n)
            n += 1
            if n == len(copies):
                for a in range(slots):
                    fetch(a).start()
            form(own, vectors, tile, group, k, 16)
        size = (lines[g + 1] - lines[g]) * width
        weights = s_ref[:, lines[g] * width : lines[g + 1] * width]
        batch = min(16, late)

        def apply(at, carry, group=group, size=size, weights=weights):
            for q in range(batch):
                a = at * batch + q
                value = lax.dot_general(
                    weights, tile[a, :size], NN, preferred_element_type=jnp.float32
                )
                if group is order[0]:
                    total[early + a] = value
                else:
                    total[early + a] += value
            return carry

        lax.fori_loop(0, late // batch, apply, 0)

    def rest(at, carry):
        a = 2 * at
        fetch(a).wait()
        fetch(a + 1).wait()
        both = jnp.concatenate([ring[lax.rem(a, slots)], ring[lax.rem(a + 1, slots)]], axis=1)
        value = lax.dot_general(s_ref[...], both, NN, preferred_element_type=jnp.float32)
        total[a] = value[:, :width]
        total[a + 1] = value[:, width:]
        pl.when(a + slots < early)(lambda: fetch(a + slots).start())
        pl.when(a + 1 + slots < early)(lambda: fetch(a + 1 + slots).start())
        return carry

    lax.fori_loop(0, early // 2, rest, 0)
    out_ref[...] = jnp.swapaxes(total[...], 0, 1).astype(out_ref.dtype)


def ladder(cholesky, tile, weights, start, rows):
    width, _, depth = cholesky.shape
    early = tile.shape[0]
    late = rows - early
    pairs, size = weights.shape
    slots = min(early, 8)
    return pl.pallas_call(
        functools.partial(ladder_kernel, early),
        out_shape=jax.ShapeDtypeStruct((pairs, rows, width), jnp.bfloat16),
        grid_spec=pltpu.PrefetchScalarGridSpec(
            num_scalar_prefetch=1,
            grid=(),
            in_specs=[ANY, ANY, VMEM],
            out_specs=VMEM,
            scratch_shapes=[
                pltpu.VMEM((width, width, depth), jnp.bfloat16),
                pltpu.VMEM((late, width, depth), jnp.bfloat16),
                pltpu.VMEM((late, GROUP * width, width), jnp.bfloat16),
                pltpu.VMEM((slots, size, width), jnp.bfloat16),
                pltpu.VMEM((rows, pairs, width), jnp.float32),
                pltpu.SemaphoreType.DMA((width // GROUP + 1,)),
                pltpu.SemaphoreType.DMA((slots,)),
            ],
        ),
        compiler_params=pltpu.CompilerParams(vmem_limit_bytes=62 << 20),
        cost_estimate=pl.CostEstimate(
            flops=2 * width * size * (late * depth + rows * pairs),
            bytes_accessed=2 * width * width * depth + 2 * early * size * width,
            transcendentals=0,
        ),
    )(start, cholesky, tile, weights)


def collected(sums):
    count_i, count_j = lax.axis_size("pi"), lax.axis_size("pj")
    landed = lax.all_to_all(sums, BOTH, split_axis=0, concat_axis=0, tiled=True)
    landed = landed.reshape((count_i, count_j, -1) + landed.shape[1:]).astype(jnp.float32)
    return jnp.sum(landed, axis=1)


def shards(amplitudes, cholesky, other_terms):
    width = cholesky.shape[0]
    pair_i, pair_j = amplitudes.shape[:2]
    count_i, count_j = lax.axis_size("pi"), lax.axis_size("pj")
    devices = count_i * count_j
    assert pair_j == 1 and pair_i * count_i == count_j
    rows = width // count_i
    early = rows // 2
    start = (lax.axis_index("pi") * rows).reshape(1)
    copies = packed_copies(amplitudes.reshape(pair_i, width, width), devices)
    weights = lax.all_to_all(copies, BOTH, split_axis=0, concat_axis=0, tiled=True)
    weights = weights.reshape(devices * pair_i, -1)
    tile = tiles(cholesky, start, early)
    part = collected(ladder(cholesky, tile, weights, start, rows))
    part = jnp.swapaxes(part, 0, 1).reshape(pair_i, width, width)
    half = other_terms.reshape(pair_i, width, width) + 0.5 * part
    back = mirrored(half.astype(jnp.bfloat16))
    total = half + jnp.swapaxes(back, 1, 2).astype(jnp.float32)
    return total.reshape(other_terms.shape)


def solution(mesh):
    return jax.shard_map(
        shards,
        mesh=mesh,
        in_specs=(P("pi", "pj", None, None), P(None, None, "pj"), P("pi", "pj", None, None)),
        out_specs=P("pi", "pj", None, None),
        check_vma=False,
    )
```

```python
import functools

import jax
import jax.numpy as jnp
from jax import lax
from jax.experimental import pallas as pl
from jax.experimental.pallas import tpu as pltpu
from jax.sharding import PartitionSpec as P


BOTH = ("pi", "pj")
GROUP = 16
NT = (((1,), (1,)), ((), ()))
NN = (((1,), (0,)), ((), ()))
ANY = pl.BlockSpec(memory_space=pl.ANY)
VMEM = pl.BlockSpec(memory_space=pltpu.VMEM)


def exchanged(block):
    pair_i = block.shape[0]
    count_i, count_j = lax.axis_size("pi"), lax.axis_size("pj")
    col = lax.axis_index("pj")
    own, arrived = [], []
    for shift in range(pair_i):
        route = []
        for row in range(count_i):
            for at in range(count_j):
                to = (at // pair_i) * count_j + pair_i * row + (at + shift) % pair_i
                route.append((row * count_j + at, to))
        sent = lax.dynamic_index_in_dim(block, (col + shift) % pair_i, 0, keepdims=False)
        own.append(sent)
        arrived.append(lax.ppermute(sent, BOTH, route))
    return own, arrived


def mirrored(block):
    pair_i = block.shape[0]
    stacked = jnp.stack(exchanged(block)[1])
    col = lax.axis_index("pj")
    return jnp.stack(
        [
            lax.dynamic_index_in_dim(stacked, (col - slot) % pair_i, 0, keepdims=False)
            for slot in range(pair_i)
        ]
    )


def groups(width):
    blocks = width // GROUP
    middle = (blocks - 2) // 2
    return [(blocks - 1,)] + [(k, blocks - 2 - k) for k in range(middle)] + [(middle,)]


def group_rows(width):
    at = [0]
    for group in groups(width):
        at.append(at[-1] + GROUP * GROUP * sum(k + 1 for k in group) // width)
    return at


def place(width, group, k, d):
    high = GROUP * (k + 1)
    if len(group) == 2:
        return d * width + (0 if k == group[0] else width - high)
    wrap = GROUP * high // width
    return d % wrap * width + d // wrap * high


def chosen(refs, which):
    value = refs[0][...].astype(jnp.float32)
    for m in range(1, len(refs)):
        value = jnp.where(which == m, refs[m][...].astype(jnp.float32), value)
    return value


def pack_kernel(pair_i, col_ref, *refs):
    own, arrived = refs[:pair_i], refs[pair_i : 2 * pair_i]
    out_ref, packed = refs[2 * pair_i :]
    width = own[0].shape[0]
    turn = lax.rem(col_ref[0], pair_i)
    d = lax.broadcasted_iota(jnp.int32, (width, width), 0)
    c = lax.broadcasted_iota(jnp.int32, (width, width), 1)
    weight = jnp.where(c < d, 1.0, jnp.where(c == d, 0.5, 0.0)).astype(jnp.float32)
    rows = group_rows(width)
    for slot in range(pair_i):
        mine = chosen(own, lax.rem(slot - turn + pair_i, pair_i))
        back = chosen(arrived, lax.rem(turn - slot + pair_i, pair_i))
        total = (jnp.swapaxes(mine, 0, 1) + back) * weight
        for g, group in enumerate(groups(width)):
            lines = rows[g + 1] - rows[g]
            value = 0.0
            for k in group:
                for first in range(0, GROUP, lines):
                    low = place(width, group, k, first)
                    part = total[GROUP * k + first : GROUP * k + first + lines]
                    value = value + (pltpu.roll(part, low, 1) if low else part)
            packed[slot, rows[g] : rows[g + 1]] = value
    final = packed[...].astype(jnp.bfloat16)

    def copy(at, carry):
        out_ref[at] = final
        return carry

    lax.fori_loop(0, out_ref.shape[0], copy, 0)


def packed_copies(pairs, devices):
    pair_i, width, _ = pairs.shape
    lines = group_rows(width)[-1]
    own, arrived = exchanged(pairs)
    return pl.pallas_call(
        functools.partial(pack_kernel, pair_i),
        out_shape=jax.ShapeDtypeStruct((devices, pair_i, lines, width), jnp.bfloat16),
        in_specs=[pl.BlockSpec(memory_space=pltpu.SMEM)] + [VMEM] * (2 * pair_i),
        out_specs=VMEM,
        scratch_shapes=[pltpu.VMEM((pair_i, lines, width), jnp.float32)],
        compiler_params=pltpu.CompilerParams(vmem_limit_bytes=40 << 20),
    )(lax.axis_index("pj").reshape(1), *own, *arrived)


AHEAD = 3


def loads(start, rows, l_hbm, own, vectors, sems, order):
    width = vectors.shape[0]
    first = pltpu.make_async_copy(l_hbm.at[pl.ds(start, rows)], own, sems.at[width // GROUP])
    copies = []
    for k in [k for group in order for k in group]:
        part = pl.ds(k * GROUP, GROUP)
        copies.append(pltpu.make_async_copy(l_hbm.at[part], vectors.at[part], sems.at[k]))
    first.start()
    for copy in copies[:2]:
        copy.start()
    first.wait()
    return copies


def arrive(copies, n):
    copies[n].wait()
    for copy in copies[2 : 1 + AHEAD] if n == 0 else copies[n + AHEAD : n + AHEAD + 1]:
        copy.start()


def form(own, vectors, tile, group, k, most):
    rows, width, depth = own.shape
    high = GROUP * (k + 1)
    chunk = min(16 if 2 * high <= width else most, rows)

    def step(at, carry):
        if chunk == rows:
            left = own[:, :high, :]
            part = slice(None)
        else:
            part = pl.ds(pl.multiple_of(at * chunk, chunk), chunk)
            left = own[part, :high, :]
        left = left.reshape(chunk * high, depth)
        for d in range(0, GROUP, 2):
            right = vectors[pl.ds(k * GROUP + d, 2)].reshape(2 * width, depth)
            product = lax.dot_general(left, right, NT, preferred_element_type=jnp.float32)
            product = product.astype(jnp.bfloat16)
            for q in range(2):
                value = product[:, q * width : (q + 1) * width].reshape(chunk, high, width)
                tile[part, pl.ds(place(width, group, k, d + q), high)] = value
        return carry

    if chunk == rows:
        step(0, 0)
    else:
        lax.fori_loop(0, rows // chunk, step, 0)


def tile_kernel(start_ref, l_hbm, t_hbm, vectors, own, tile, sems, sent):
    rows, width, _ = own.shape
    lines = group_rows(width)
    copies = loads(start_ref[0], rows, l_hbm, own, vectors, sems, groups(width))
    n = 0
    outs = []
    for g, group in enumerate(groups(width)):
        if g >= 2:
            outs[g - 2].wait()
        for k in group:
            arrive(copies, n)
            n += 1
            form(own, vectors, tile.at[g % 2], group, k, 8)
        low, size = lines[g] * width, (lines[g + 1] - lines[g]) * width
        outs.append(
            pltpu.make_async_copy(
                tile.at[g % 2, :, pl.ds(0, size)], t_hbm.at[:, pl.ds(low, size)], sent.at[g % 2]
            )
        )
        outs[g].start()
    for copy in outs[-2:]:
        copy.wait()


def tiles(cholesky, start, rows):
    width, _, depth = cholesky.shape
    size = group_rows(width)[-1] * width
    return pl.pallas_call(
        tile_kernel,
        out_shape=jax.ShapeDtypeStruct((rows, size, width), jnp.bfloat16),
        grid_spec=pltpu.PrefetchScalarGridSpec(
            num_scalar_prefetch=1,
            grid=(),
            in_specs=[ANY],
            out_specs=ANY,
            scratch_shapes=[
                pltpu.VMEM((width, width, depth), jnp.bfloat16),
                pltpu.VMEM((rows, width, depth), jnp.bfloat16),
                pltpu.VMEM((2, rows, GROUP * width, width), jnp.bfloat16),
                pltpu.SemaphoreType.DMA((width // GROUP + 1,)),
                pltpu.SemaphoreType.DMA((2,)),
            ],
        ),
        compiler_params=pltpu.CompilerParams(vmem_limit_bytes=60 << 20),
        cost_estimate=pl.CostEstimate(
            flops=2 * rows * width * size * depth,
            bytes_accessed=2 * width * width * depth + 2 * rows * size * width,
            transcendentals=0,
        ),
    )(start, cholesky)


def ladder_kernel(
    early, start_ref, l_hbm, t_hbm, s_ref, out_ref, vectors, own, tile, ring, total, sems, got
):
    late, width, _ = own.shape
    slots = ring.shape[0]
    lines = group_rows(width)
    order = groups(width)
    order = order[1:] + order[:1]
    copies = loads(start_ref[0] + early, late, l_hbm, own, vectors, sems, order)

    def fetch(a):
        slot = lax.rem(a, slots)
        return pltpu.make_async_copy(t_hbm.at[a], ring.at[slot], got.at[slot])

    n = 0
    for group in order:
        g = groups(width).index(group)
        for k in group:
            arrive(copies, n)
            n += 1
            if n == len(copies):
                for a in range(slots):
                    fetch(a).start()
            form(own, vectors, tile, group, k, 16)
        size = (lines[g + 1] - lines[g]) * width
        weights = s_ref[:, lines[g] * width : lines[g + 1] * width]
        batch = min(16, late)

        def apply(at, carry, group=group, size=size, weights=weights):
            for q in range(batch):
                a = at * batch + q
                value = lax.dot_general(
                    weights, tile[a, :size], NN, preferred_element_type=jnp.float32
                )
                if group is order[0]:
                    total[early + a] = value
                else:
                    total[early + a] += value
            return carry

        lax.fori_loop(0, late // batch, apply, 0)

    def rest(at, carry):
        a = 2 * at
        fetch(a).wait()
        fetch(a + 1).wait()
        both = jnp.concatenate([ring[lax.rem(a, slots)], ring[lax.rem(a + 1, slots)]], axis=1)
        value = lax.dot_general(s_ref[...], both, NN, preferred_element_type=jnp.float32)
        total[a] = value[:, :width]
        total[a + 1] = value[:, width:]
        pl.when(a + slots < early)(lambda: fetch(a + slots).start())
        pl.when(a + 1 + slots < early)(lambda: fetch(a + 1 + slots).start())
        return carry

    lax.fori_loop(0, early // 2, rest, 0)
    out_ref[...] = jnp.swapaxes(total[...], 0, 1).astype(out_ref.dtype)


def ladder(cholesky, tile, weights, start, rows):
    width, _, depth = cholesky.shape
    early = tile.shape[0]
    late = rows - early
    pairs, size = weights.shape
    slots = min(early, 8)
    return pl.pallas_call(
        functools.partial(ladder_kernel, early),
        out_shape=pltpu.VMEM((pairs, rows, width), jnp.bfloat16),
        grid_spec=pltpu.PrefetchScalarGridSpec(
            num_scalar_prefetch=1,
            grid=(),
            in_specs=[ANY, ANY, VMEM],
            out_specs=VMEM,
            scratch_shapes=[
                pltpu.VMEM((width, width, depth), jnp.bfloat16),
                pltpu.VMEM((late, width, depth), jnp.bfloat16),
                pltpu.VMEM((late, GROUP * width, width), jnp.bfloat16),
                pltpu.VMEM((slots, size, width), jnp.bfloat16),
                pltpu.VMEM((rows, pairs, width), jnp.float32),
                pltpu.SemaphoreType.DMA((width // GROUP + 1,)),
                pltpu.SemaphoreType.DMA((slots,)),
            ],
        ),
        compiler_params=pltpu.CompilerParams(vmem_limit_bytes=58 << 20),
        cost_estimate=pl.CostEstimate(
            flops=2 * width * size * (late * depth + rows * pairs),
            bytes_accessed=2 * width * width * depth + 2 * early * size * width,
            transcendentals=0,
        ),
    )(start, cholesky, tile, weights)


def collected(sums):
    count_i, count_j = lax.axis_size("pi"), lax.axis_size("pj")
    landed = lax.all_to_all(sums, BOTH, split_axis=0, concat_axis=0, tiled=True)
    landed = landed.reshape((count_i, count_j, -1) + landed.shape[1:]).astype(jnp.float32)
    return jnp.sum(landed, axis=1)


def shards(amplitudes, cholesky, other_terms):
    width = cholesky.shape[0]
    pair_i, pair_j = amplitudes.shape[:2]
    count_i, count_j = lax.axis_size("pi"), lax.axis_size("pj")
    devices = count_i * count_j
    assert pair_j == 1 and pair_i * count_i == count_j
    rows = width // count_i
    early = rows // 2
    start = (lax.axis_index("pi") * rows).reshape(1)
    copies = packed_copies(amplitudes.reshape(pair_i, width, width), devices)
    weights = lax.all_to_all(copies, BOTH, split_axis=0, concat_axis=0, tiled=True)
    weights = weights.reshape(devices * pair_i, -1)
    if weights.size <= 1 << 20:
        weights = pltpu.with_memory_space_constraint(weights, pltpu.VMEM)
    tile = tiles(cholesky, start, early)
    part = collected(ladder(cholesky, tile, weights, start, rows))
    part = jnp.swapaxes(part, 0, 1).reshape(pair_i, width, width)
    half = other_terms.reshape(pair_i, width, width) + 0.5 * part
    back = mirrored(half.astype(jnp.bfloat16))
    total = half + jnp.swapaxes(back, 1, 2).astype(jnp.float32)
    return total.reshape(other_terms.shape)


def solution(mesh):
    return jax.shard_map(
        shards,
        mesh=mesh,
        in_specs=(P("pi", "pj", None, None), P(None, None, "pj"), P("pi", "pj", None, None)),
        out_specs=P("pi", "pj", None, None),
        check_vma=False,
    )
```
